32 devices in a mesh: space: 8 (over z, y), mem: 4 (over x, core).
Axes of the slice: x: 2, y: 2, z: 4, core: 2. Of those that a mesh axis runs over, the one named last changes fastest.
Arguments:
- background_sample_fields: float32 [2560, 8192], P('mem', 'space'), may hold values from -20 to 20, as said below
- cfl_ratio: float32 [8192], P('space'), may hold values from 0.3 to 0.95
- eigvec: bfloat16 [2560, 2560], P('mem'), may hold values from -0.125 to 0.125
- eigval: float32 [2560], replicated, may hold values from 26 to 51200
- innov: float32 [2560], P('mem'), may hold values from -640 to 640
Outputs:
- analysis: float32 [2560, 8192], P('mem', 'space')
The draws below stay inside these ranges and needn't reach their ends.
Inputs may be any that keep to these rules, and one draw needn't show every extreme that they name: `background_sample_fields`: a common state plus a member perturbation.
All inputs are finite; a program needn't handle non-finite values.
Results may differ from the reference program's by a relative error of at most 0.0003.
Values may be sent and summed in bfloat16 or wider, within the bound.
No kernel may reach another device: no remote copies, remote signals or barrier semaphores. Data moves between devices by JAX's collectives and lax.ppermute only.
A program may use at most 64 MiB of HBM per device.

```python
import math
import jax
import jax.numpy as jnp
from jax import lax

REPLICA_NUMBER = 2560
NX = 8192


def draw_background_sample_fields(key, part):
    key_base = jax.random.fold_in(key, 11)
    key_pert = jax.random.fold_in(key, 12)
    base = jnp.clip(2.0 * jax.random.normal(key_base, (NX,), jnp.float32), -8.0, 8.0)
    pert = jnp.clip(jax.random.normal(key_pert, (REPLICA_NUMBER, NX), jnp.float32), -6.0, 6.0)
    return base[None, :] + pert


def shard_levels(stream_key, dims, split, low, high):
    factor_of = 1.0
    for axis_at, parts in split:
        steps = jax.random.uniform(jax.random.fold_in(jax.random.fold_in(stream_key, 6), axis_at), (parts,), jnp.float32, low / len(split), high / len(split))
        factor_of = factor_of * jnp.repeat(jnp.exp(steps), dims[axis_at] // parts).reshape((-1,) + (1,) * (len(dims) - 1 - axis_at))
    return factor_of


def gaussian(rng, shape, scale, most, split=(), kind=jnp.bfloat16):
    drawn = jax.random.normal(rng, shape, jnp.float32) * scale
    if len(split) > 0:
        drawn = shard_levels(rng, shape, split, -0.22, 0.18) * drawn
    return jnp.clip(drawn, min=-most, max=most).astype(kind)


def setup_inputs(seed: int = 0) -> dict:
    splits = jax.random.split(jax.random.key(seed), 6)
    return {
        "background_sample_fields": draw_background_sample_fields(jax.random.fold_in(splits[5], 71), 0),
        "cfl_ratio": jnp.clip(0.3 + 0.65 * jax.random.uniform(splits[1], (NX,), jnp.float32) ** shard_levels(splits[1], (NX,), ((0, 8),), -0.2, 0.2), 0.3, 0.95),
        "eigvec": gaussian(splits[2], (REPLICA_NUMBER, REPLICA_NUMBER), REPLICA_NUMBER ** -0.5, 0.125, ((0, 4),)),
        "eigval": jnp.clip(jnp.exp(jax.random.uniform(splits[3], (REPLICA_NUMBER,), jnp.float32, math.log(26.0), math.log(51200.0))), 26.0, 51200.0),
        "innov": gaussian(splits[4], (REPLICA_NUMBER,), (REPLICA_NUMBER // 25 + 1), 640.0, ((0, 4),), jnp.float32),
    }


def reference(background_sample_fields, cfl_ratio, eigvec, eigval, innov):
    high = lax.Precision.HIGHEST
    upwind_adjacent = jnp.roll(background_sample_fields, 1, axis=1)
    downwind_adjacent = jnp.roll(background_sample_fields, -1, axis=1)
    predicted_fields = background_sample_fields - 0.5 * cfl_ratio * (downwind_adjacent - upwind_adjacent) + 0.5 * cfl_ratio * cfl_ratio * (downwind_adjacent - 2.0 * background_sample_fields + upwind_adjacent)
    sample_centroid = lax.optimization_barrier(jnp.sum(predicted_fields, axis=0)) / REPLICA_NUMBER
    deviation_table = predicted_fields - sample_centroid
    vecs = eigvec.astype(jnp.float32)
    proj = jnp.dot(innov, vecs, precision=high)
    denom = eigval + (REPLICA_NUMBER - 1.0)
    wbar = jnp.dot(vecs, proj / denom, precision=high)
    shift = jnp.dot(wbar, deviation_table, precision=high)
    gain = jnp.sqrt((REPLICA_NUMBER - 1.0) / denom)
    coef = jnp.dot(vecs.T, deviation_table, precision=high)
    mixed = jnp.dot(vecs, gain[:, None] * coef, precision=high)
    return sample_centroid + shift + mixed
```

```python
import functools

import jax
import jax.numpy as jnp
from jax import lax
from jax.experimental import pallas as pl
from jax.experimental.pallas import tpu as pltpu
from jax.sharding import PartitionSpec as P

F32 = jnp.float32
BF16 = jnp.bfloat16
VALUE_SCALE = 512.0


def params(mib):
    return pltpu.CompilerParams(vmem_limit_bytes=mib << 20)


def encode(u):
    u2 = u * u
    u4 = u2 * u2
    u8 = u4 * u4
    return jnp.where(u < 0, -u8, u8).astype(BF16)


def decode(code, scale):
    v = code.astype(F32)
    a = jnp.sqrt(jnp.sqrt(jnp.sqrt(jnp.abs(v)))) * scale
    return jnp.where(v < 0, -a, a)


def split(x):
    hi = x.astype(BF16)
    return hi, (x - hi.astype(F32)).astype(BF16)


def rows3(x):
    a = x.astype(BF16).astype(F32)
    b = (x - a).astype(BF16).astype(F32)
    c = x - a - b
    row = lax.broadcasted_iota(jnp.int32, (16, x.shape[1]), 0)
    zero = jnp.zeros((16, x.shape[1]), F32)
    out = jnp.where(row == 0, a, jnp.where(row == 1, b, jnp.where(row == 2, c, zero)))
    return out.astype(BF16)


def mm(a, b):
    return jnp.dot(a, b, preferred_element_type=F32)


def mm_t(a, b):
    return lax.dot_general(a, b, (((1,), (1,)), ((), ())), preferred_element_type=F32)


def whole(count):
    return [pl.BlockSpec(memory_space=pltpu.VMEM)] * count


def prep_kernel(v_ref, g_ref, innov_ref, hi_ref, lo_ref, proj_ref):
    rows = v_ref.shape[0]

    def body(i, carry):
        at = pl.ds(pl.multiple_of(i * 16, 16), 16)
        hi, lo = split(v_ref[at, :].astype(F32) * g_ref[...])
        hi_ref[at, :] = hi
        lo_ref[at, :] = lo
        return carry

    lax.fori_loop(0, rows // 16, body, 0)
    proj_ref[...] = jnp.sum(mm(rows3(innov_ref[...]), v_ref[...]), axis=0, keepdims=True)


def prep(v, g, innov):
    return pl.pallas_call(
        prep_kernel,
        out_shape=(
            jax.ShapeDtypeStruct(v.shape, BF16),
            jax.ShapeDtypeStruct(v.shape, BF16),
            jax.ShapeDtypeStruct(g.shape, F32),
        ),
        in_specs=whole(3),
        out_specs=tuple(whole(3)),
        compiler_params=params(24),
        name="prep",
    )(v, g, innov)


def forecast_kernel(chunks, b_ref, left_ref, right_ref, c_ref, f_ref, full_ref, mean_ref, *chunk_refs):
    rows, width = b_ref.shape
    c = c_ref[...]
    c1 = 0.5 * c
    c2 = 0.5 * c * c
    lane = lax.broadcasted_iota(jnp.int32, (16, width), 1)

    def first(i, acc):
        at = pl.ds(pl.multiple_of(i * 16, 16), 16)
        x = b_ref[at, :]
        up = jnp.where(lane == 0, left_ref[at, :], pltpu.roll(x, 1, 1))
        down = jnp.where(lane == width - 1, right_ref[at, :], pltpu.roll(x, width - 1, 1))
        f = x - c1 * (down - up) + c2 * (down - 2.0 * x + up)
        f_ref[at, :] = f
        return acc + f

    acc = lax.fori_loop(0, rows // 16, first, jnp.zeros((16, width), F32))
    mean = jnp.sum(acc, axis=0, keepdims=True) / rows
    mean_ref[...] = mean

    def second(i, carry):
        at = pl.ds(pl.multiple_of(i * 16, 16), 16)
        code = encode((f_ref[at, :] - mean) * VALUE_SCALE)
        full_ref[at, :] = code
        for ref, (start, size) in zip(chunk_refs, chunks):
            ref[at, :] = code[:, start : start + size]
        return carry

    lax.fori_loop(0, rows // 16, second, 0)


def forecast(b, left, right, c, chunks):
    rows, width = b.shape
    return pl.pallas_call(
        functools.partial(forecast_kernel, chunks),
        out_shape=(
            jax.ShapeDtypeStruct(b.shape, F32),
            jax.ShapeDtypeStruct(b.shape, BF16),
            jax.ShapeDtypeStruct((1, width), F32),
            *(jax.ShapeDtypeStruct((rows, size), BF16) for _, size in chunks),
        ),
        in_specs=whole(4),
        out_specs=tuple(whole(3 + len(chunks))),
        compiler_params=params(24),
        name="forecast",
    )(b, left, right, c)


def shift_kernel(q_ref, v_ref, f_ref, mean_ref, out_ref):
    wbar = jnp.sum(mm_t(rows3(q_ref[...]), v_ref[...]), axis=0, keepdims=True)
    w3 = rows3(wbar)
    width = f_ref.shape[1]
    mean = mean_ref[...]
    row = lax.broadcasted_iota(jnp.int32, (8, 256), 0)
    total = jnp.sum(wbar)
    for start in range(0, width, 256):
        at = slice(start, start + 256)
        hi, lo = split(f_ref[:, at] - mean[:, at])
        s = jnp.sum(mm(w3, hi) + mm(w3, lo), axis=0, keepdims=True)
        out_ref[:, at] = jnp.where(row == 0, mean[:, at], jnp.where(row == 1, s, total))


def shift_part(q, v, f, mean):
    return pl.pallas_call(
        shift_kernel,
        out_shape=jax.ShapeDtypeStruct((8, f.shape[1]), F32),
        in_specs=whole(4),
        out_specs=whole(1)[0],
        compiler_params=params(24),
        name="shift",
    )(q, v, f, mean)


def cross_kernel(scale_ref, a_ref, b_ref, hi_ref, lo_ref, out_ref):
    v = jnp.concatenate([a_ref[...], b_ref[...]], axis=0)
    t = mm_t(v, hi_ref[...]) + mm_t(v, lo_ref[...])
    out_ref[...] = encode(t * scale_ref[0])


def cross(scale, a, b, hi, lo):
    return pl.pallas_call(
        cross_kernel,
        out_shape=jax.ShapeDtypeStruct((2 * a.shape[0], hi.shape[0]), BF16),
        in_specs=[pl.BlockSpec(memory_space=pltpu.SMEM)] + whole(4),
        out_specs=whole(1)[0],
        compiler_params=params(24),
        name="cross",
    )(scale, a, b, hi, lo)


def gram_kernel(hi_ref, lo_ref, v_ref, th_ref, tl_ref):
    v = v_ref[...]
    th_ref[...], tl_ref[...] = split(mm_t(hi_ref[...], v) + mm_t(lo_ref[...], v))


def gram(hi, lo, v):
    shape = jax.ShapeDtypeStruct((hi.shape[0], v.shape[0]), BF16)
    return pl.pallas_call(
        gram_kernel,
        out_shape=(shape, shape),
        in_specs=whole(3),
        out_specs=tuple(whole(2)),
        compiler_params=params(28),
        name="gram",
    )(hi, lo, v)


def mm3(ah, al, p):
    ph, pl_ = split(p)
    return mm(ah, ph) + mm(al, ph) + mm(ah, pl_)


def local_kernel(oh, ol, sh, sl, f_ref, code_ref, xbar_ref, d_ref, out_ref):
    own = mm3(oh[...], ol[...], f_ref[...] - xbar_ref[...])
    sib = mm3(sh[...], sl[...], decode(code_ref[...], 1.0 / VALUE_SCALE) + d_ref[...])
    out_ref[...] = own + sib


def local(own, sib, f, code, xbar, d):
    rows, width = f.shape
    col = lambda j: (0, j)
    fixed = pl.BlockSpec((rows, rows), lambda j: (0, 0))
    block = pl.BlockSpec((rows, 256), col)
    line = pl.BlockSpec((1, 256), col)
    return pl.pallas_call(
        local_kernel,
        out_shape=jax.ShapeDtypeStruct(f.shape, F32),
        grid=(width // 256,),
        in_specs=[fixed] * 4 + [block, block, line, line],
        out_specs=block,
        compiler_params=params(24),
        name="local",
    )(*own, *sib, f, code, xbar, d)


def place_kernel(count, order_ref, scale_ref, *refs):
    blocks = refs[:count]
    hi_ref, lo_ref, t_ref = refs[count:]
    half = blocks[0].shape[0] // 2
    rows = t_ref.shape[0] // 2
    for n, ref in enumerate(blocks):
        t = decode(ref[...], scale_ref[0])
        base = pl.multiple_of(order_ref[n] * half, half)
        t_ref[pl.ds(base, half), :] = t[:half]
        t_ref[pl.ds(rows + base, half), :] = t[half:]
    for start in range(0, 2 * rows, 128):
        stop = min(start + 128, 2 * rows)
        hi, lo = split(t_ref[start:stop, :].T)
        hi_ref[:, start:stop] = hi
        lo_ref[:, start:stop] = lo


def place(order, scale, blocks):
    count = len(blocks)
    both = count * blocks[0].shape[0]
    rows = blocks[0].shape[1]
    shape = jax.ShapeDtypeStruct((rows, both), BF16)
    return pl.pallas_call(
        functools.partial(place_kernel, count),
        out_shape=(shape, shape),
        in_specs=[pl.BlockSpec(memory_space=pltpu.SMEM)] * 2 + whole(count),
        out_specs=tuple(whole(2)),
        scratch_shapes=[pltpu.VMEM((both, rows), F32)],
        compiler_params=params(24),
        name="place",
    )(order, scale, *blocks)


def final_kernel(count, base_ref, y_ref, *refs):
    out_ref = refs[-1]
    acc = y_ref[...] + base_ref[...]
    rows = y_ref.shape[0]
    for n in range(count):
        hi, lo, ca, cb, da, db = refs[6 * n : 6 * n + 6]
        inv = 1.0 / VALUE_SCALE
        p = jnp.concatenate([decode(ca[...], inv) + da[...], decode(cb[...], inv) + db[...]], axis=0)
        acc = acc + mm3(hi[...], lo[...], p)
    out_ref[...] = acc


def final(base, y, parts, start, size):
    rows = y.shape[0]
    at = start // size
    block = pl.BlockSpec((rows, size), lambda i: (0, at))
    line = pl.BlockSpec((1, size), lambda i: (0, at))
    code = pl.BlockSpec((rows, size), lambda i: (0, 0))
    mat = pl.BlockSpec((rows, 2 * rows), lambda i: (0, 0))
    return pl.pallas_call(
        functools.partial(final_kernel, len(parts)),
        out_shape=jax.ShapeDtypeStruct(y.shape, F32),
        grid=(1,),
        in_specs=[line, block] + [mat, mat, code, code, line, line] * len(parts),
        out_specs=block,
        input_output_aliases={1: 0},
        compiler_params=params(40),
        name="final",
    )(base, y, *(a for part in parts for a in part))


def ring_of(count):
    return [2 * i for i in range(count // 2)] + [2 * i + 1 for i in reversed(range(count // 2))]


def per_device(b, c, v, eigval, innov):
    members, spaces = lax.axis_size("mem"), lax.axis_size("space")
    m, s = lax.axis_index("mem"), lax.axis_index("space")
    rows, total = v.shape
    width = b.shape[1]
    outer = members // 2
    swap = [(i, i ^ 1) for i in range(members)]
    hops = [[(i, (i + 2 * o) % members) for i in range(members)] for o in range(1, outer)]
    sends = functools.partial(lax.ppermute, axis_name="mem")

    parts = spaces
    while parts > 1 and (rows % parts or (rows // parts) % 16):
        parts //= 2
    part_rows = rows // parts
    mine = s % parts

    v_part = lax.dynamic_slice_in_dim(v, mine * part_rows, part_rows, 0)
    far_v = [sends(v_part, perm=hop) for hop in hops]
    sib_v = sends(v, perm=swap)

    up = [(i, (i + 1) % spaces) for i in range(spaces)]
    down = [(j, i) for i, j in up]
    left = lax.ppermute(b[:, width - 1].reshape(1, rows), "space", up).reshape(rows, 1)
    right = lax.ppermute(b[:, 0].reshape(1, rows), "space", down).reshape(rows, 1)

    denom = eigval + (total - 1.0)
    gain = jnp.sqrt((total - 1.0) / denom)
    bound = jnp.sum(gain) / 64.0
    hi, lo, proj = prep(v, gain.reshape(1, total), innov.reshape(1, rows))
    proj = proj + sends(proj, perm=swap)
    proj = proj + sum(sends(proj, perm=hop) for hop in hops)

    size = 256
    chunks = [(i, size) for i in range(0, width, size)]
    f, code, mean, *code_chunks = forecast(b, left, right, c.reshape(1, width), chunks)

    sib_v_part = [sends(a, perm=swap) for a in far_v]
    sib_code = sends(code, perm=swap)
    far_code = [[sends(a, perm=hop) for a in code_chunks] for hop in hops]
    far_sib_code = [[sends(a, perm=swap) for a in far] for far in far_code]

    stats = shift_part(proj / denom.reshape(1, total), v, f, mean)
    pair = jnp.concatenate([stats, sends(stats, perm=swap)], axis=0)
    far_pairs = [sends(pair, perm=hop) for hop in hops]
    every = [p[i : i + 8] for p in [pair, *far_pairs] for i in (0, 8)]
    xbar = sum(e[0:1] for e in every) / members
    offsets = [e[0:1] - xbar for e in every]
    base = xbar + sum(e[1:2] + e[2:3] * d for e, d in zip(every, offsets))

    ring = ring_of(parts) if parts > 1 else [0]
    place_of = [ring.index(i) for i in range(parts)]
    groups = range(0, spaces, parts)
    ahead = [(g + ring[i], g + ring[(i + 1) % parts]) for g in groups for i in range(parts)]
    behind = [(j, i) for i, j in ahead]
    at = jnp.asarray(place_of, jnp.int32)[mine]
    walk = jnp.asarray(ring, jnp.int32)
    to_code, to_value = (32768.0 / bound).reshape(1), (bound / 32768.0).reshape(1)
    far_t = []
    for a, a_sib in zip(far_v, sib_v_part):
        own = cross(to_code, a, a_sib, hi, lo)
        blocks, order = [own], [at]
        fwd = bwd = own
        for step in range(1, parts // 2 + 1):
            fwd = lax.ppermute(fwd, "space", ahead)
            blocks.append(fwd)
            order.append((at - step) % parts)
            if step < (parts + 1) // 2:
                bwd = lax.ppermute(bwd, "space", behind)
                blocks.append(bwd)
                order.append((at + step) % parts)
        far_t.append(place(walk[jnp.stack(order)], to_value, blocks))

    own_t = gram(hi, lo, v)
    sib_t = gram(hi, lo, sib_v)
    y = local(own_t, sib_t, f, sib_code, xbar, offsets[1])
    for n, (start, size) in enumerate(chunks):
        far = [
            (*t, far_code[o][n], far_sib_code[o][n], offsets[2 * o + 2], offsets[2 * o + 3])
            for o, t in enumerate(far_t)
        ]
        y = final(base, y, far, start, size)
    return y


def solution(mesh):
    in_specs = (P("mem", "space"), P("space"), P("mem", None), P(), P("mem"))
    out_specs = P("mem", "space")
    return jax.shard_map(per_device, mesh=mesh, in_specs=in_specs, out_specs=out_specs, check_vma=False)
```
